256 devices in a mesh: fsdp: 16 (over z, x_lo), tp: 8 (over y, core), rep: 2 (over x_hi).
Axes of the slice: x: 4 (x_hi: 2, x_lo: 2; x = x_hi * 2 + x_lo), y: 4, z: 8, core: 2. Of those that a mesh axis runs over, the one named last changes fastest.
Arguments:
- hidden: bfloat16 [4096, 16384], P(('rep', 'fsdp')), parts along dimension 0, may hold values from -400 to 400
- base_weight: bfloat16 [32768, 16384], P(('rep', 'fsdp', 'tp')), parts along dimension 0, may hold values from -1 to 1
- adapter_down: bfloat16 [32768, 32], P(('rep', 'fsdp', 'tp')), parts along dimension 0, may hold values from -0.046875 to 0.046875
- adapter_up: bfloat16 [64, 16384], P('rep'), parts along dimension 0, may hold values from -0.1796875 to 0.1796875
- norm_gain: bfloat16 [32768], P('rep'), parts along dimension 0, may hold values from 0.25 to 1.75
- positions: int32 [4096], P(('rep', 'fsdp')), parts along dimension 0, may hold values from 0 to 6142, as said below
Outputs:
- queries: bfloat16 [4096, 16384], P(('rep', 'fsdp'), 'tp'), parts along dimension 0
The draws below stay inside these ranges and needn't reach their ends.
There are 2 independent parts, one for each index of `rep`. The reference program is written for one: setup_inputs(seed, part) draws one part's arguments, and reference() takes and returns one part's arrays. A program takes and returns all parts, laid end to end along the dimension named above; each array names one. Nothing has to cross between parts.
Inputs may be any that keep to these rules, and one draw needn't show every extreme that they name: Within a document positions rise by one from token to token; every document after the first starts at 0; the first document continues an earlier one and its last token has position 6142.
All inputs are finite; a program needn't handle non-finite values.
Results may differ from the reference program's by a relative error of at most 0.018.
Values may be sent and summed in bfloat16 or wider, within the bound.
A program may use at most 128 MiB of HBM per device.

```python
import math
import jax
import jax.numpy as jnp
from jax import lax

D = 16384
HEAD = 128
R = 32
BLOCK = 128
TOKENS = 2048
N_FSDP = 16


def draw_hidden(key, part):
    noise_key, row_key, col_key = jax.random.split(key, 3)
    row_scale = jnp.exp(jax.random.uniform(row_key, (TOKENS, 1), jnp.float32, 0.0, math.log(10.0)))
    col_scale = jnp.exp(jax.random.uniform(col_key, (1, D), jnp.float32, 0.0, math.log(10.0)))
    noise = jnp.clip(jax.random.normal(noise_key, (TOKENS, D), jnp.float32), -4.0, 4.0)
    return (noise * row_scale * col_scale).astype(jnp.bfloat16)


def draw_base_weight(key, part):
    noise_key, row_key, col_key = jax.random.split(jax.random.fold_in(key, 7), 3)
    row_factor = jnp.exp(jax.random.uniform(row_key, (D, 1), jnp.float32, math.log(0.2), math.log(2.0)))
    col_factor = jnp.exp(jax.random.uniform(col_key, (1, D), jnp.float32, math.log(0.2), math.log(2.0)))
    noise = jnp.clip(jax.random.normal(noise_key, (D, D), jnp.float32), -4.0, 4.0)
    return (noise * row_factor * col_factor * (1.0 / math.sqrt(D))).astype(jnp.bfloat16)


def draw_positions(key, part):
    start_key, forced_key = jax.random.split(jax.random.fold_in(key, 13), 2)
    index = jnp.arange(TOKENS, dtype=jnp.int32)
    spacing = max(4, TOKENS // 8)
    forced = jax.random.randint(forced_key, (), 1, TOKENS, dtype=jnp.int32)
    starts = (jax.random.randint(start_key, (TOKENS,), 0, spacing, dtype=jnp.int32) == 0) | (index == 0) | (index == forced)
    latest = lax.cummax(jnp.where(starts, index, 0), axis=0)
    later = starts & (index > 0)
    first_length = jnp.min(jnp.where(later, index, TOKENS)).astype(jnp.int32)
    offset = (TOKENS + 4095 - first_length).astype(jnp.int32)
    return (index - latest + jnp.where(latest == 0, offset, 0)).astype(jnp.int32)


def levels(stream_key, shape, cuts, low, high):
    factor_of, own = 1.0, jax.random.fold_in(stream_key, 6)
    for position, blocks in cuts:
        heights = jnp.exp(jax.random.uniform(jax.random.fold_in(own, position), (blocks,), jnp.float32, low / len(cuts), high / len(cuts)))
        factor_of = factor_of * jnp.repeat(heights, shape[position] // blocks).reshape([-1 if axis == position else 1 for axis in range(len(shape))])
    return factor_of


def normal_values(key, dims, scale, limit, shards=(), kind=jnp.bfloat16):
    gain = levels(key, dims, shards, -0.22, 0.18) if shards else 1.0
    drawn = jax.random.normal(key, dims, jnp.float32) * scale * gain
    return jnp.minimum(jnp.maximum(drawn, -limit), limit).astype(kind)


def setup_inputs(seed: int = 0, part: int = 0) -> dict:
    keys = jax.random.split(jax.random.key(seed), 7)
    part_keys = jax.random.split(jax.random.fold_in(keys[6], part), 7)
    hidden = draw_hidden(jax.random.fold_in(jax.random.fold_in(keys[6], part), 71), part)
    base_weight = draw_base_weight(jax.random.fold_in(jax.random.fold_in(keys[6], part), 71), part)
    adapter_down = normal_values(part_keys[2], (D, R), D ** -0.5, 0.046875, ((0, 128),))
    adapter_up = normal_values(part_keys[3], (R, D), 0.03, 0.1796875)
    norm_gain = jnp.clip(1.0 + 0.15 * jax.random.normal(part_keys[4], (D,), jnp.float32), 0.25, 1.75).astype(jnp.bfloat16)
    positions = draw_positions(jax.random.fold_in(jax.random.fold_in(keys[6], part), 71), part)
    return {"hidden": hidden, "base_weight": base_weight, "adapter_down": adapter_down, "adapter_up": adapter_up, "norm_gain": norm_gain, "positions": positions}


norm_epsilon = 1e-05
scale_epsilon = 1e-06
code_limit = 15.0
adapter_scale = 2.0
rope_theta = 500000.0
rope_factor = 8.0
low_factor = 1.0
high_factor = 4.0
initial_context = 8192.0

def normalize(hidden, norm_gain):
    values = hidden.astype(jnp.float32)
    mean_square = lax.optimization_barrier(jnp.mean(values * values, axis=1, keepdims=True))
    return (values * lax.rsqrt(mean_square + norm_epsilon) * norm_gain.astype(jnp.float32)[None, :]).astype(jnp.bfloat16)

def quantize(base_rows, low_rank):
    merged = base_rows.astype(jnp.float32) + adapter_scale * low_rank
    row_count, col_count = merged.shape
    tiles = merged.reshape(row_count // BLOCK, BLOCK, col_count // BLOCK, BLOCK)
    largest = lax.optimization_barrier(jnp.max(jnp.abs(tiles), axis=(1, 3)))
    exponent = jnp.ceil(jnp.log2((largest + scale_epsilon) / code_limit))
    scales = jnp.exp2(exponent).astype(jnp.bfloat16)
    quantized = jnp.floor(tiles / scales.astype(jnp.float32)[:, None, :, None] + 0.5).astype(jnp.bfloat16)
    return (quantized.reshape(row_count, col_count), scales)

def dequantize(quantized, scales):
    row_count, col_count = quantized.shape
    tiles = quantized.reshape(row_count // BLOCK, BLOCK, col_count // BLOCK, BLOCK).astype(jnp.float32)
    return (tiles * scales.astype(jnp.float32)[:, None, :, None]).astype(jnp.bfloat16).reshape(row_count, col_count)

def frequencies(positions):
    pair_index = jnp.arange(HEAD // 2, dtype=jnp.float32)
    inverse = jnp.exp(pair_index * (-2.0 * math.log(rope_theta) / HEAD))
    wavelength = 2.0 * math.pi / inverse
    blend = (initial_context / wavelength - low_factor) / (high_factor - low_factor)
    middle = (1.0 - blend) * inverse / rope_factor + blend * inverse
    adjusted = jnp.where(wavelength < initial_context / high_factor, inverse, jnp.where(wavelength > initial_context / low_factor, inverse / rope_factor, middle))
    angles = positions.astype(jnp.float32)[:, None] * adjusted[None, :]
    return (jnp.cos(angles), jnp.sin(angles))

def rotate(projected, positions):
    cosine, sine_part = frequencies(positions)
    row_count, full_width = projected.shape
    half_head = HEAD // 2
    per_head = projected.reshape(row_count, full_width // HEAD, HEAD)
    first_half = per_head[:, :, :half_head]
    second_half = per_head[:, :, half_head:]
    cosine = cosine[:, None, :]
    sine_part = sine_part[:, None, :]
    turned = jnp.concatenate([first_half * cosine - second_half * sine_part, second_half * cosine + first_half * sine_part], axis=2)
    return turned.reshape(row_count, full_width)

def reference(hidden, base_weight, adapter_down, adapter_up, norm_gain, positions):
    normed = normalize(hidden, norm_gain)
    group_rows = D // N_FSDP

    def one_group(carry, group_index):
        first_row = (group_index * group_rows).astype(jnp.int32)
        base_rows = lax.dynamic_slice_in_dim(base_weight, first_row, group_rows, 0)
        down_rows = lax.dynamic_slice_in_dim(adapter_down, first_row, group_rows, 0)
        input_cols = lax.dynamic_slice_in_dim(normed, first_row, group_rows, 1)
        low_rank = jnp.dot(down_rows, adapter_up, preferred_element_type=jnp.float32)
        quantized, scales = quantize(base_rows, low_rank)
        weight = dequantize(quantized, scales)
        partial_value = jnp.dot(input_cols, weight, preferred_element_type=jnp.float32)
        partial_value = lax.optimization_barrier(partial_value.astype(jnp.bfloat16)).astype(jnp.float32)
        return (carry + partial_value, None)
    projected, _ = lax.scan(one_group, jnp.zeros((TOKENS, D), jnp.float32), jnp.arange(N_FSDP, dtype=jnp.int32))
    return rotate(projected, positions).astype(jnp.bfloat16)
```

```python
import functools
import math

import jax
import jax.numpy as jnp
from jax import lax
from jax.experimental import pallas as pl
from jax.experimental.pallas import tpu as pltpu
from jax.sharding import PartitionSpec as P

HEAD = 128
BLOCK = 128
F32 = jnp.float32
BF16 = jnp.bfloat16

norm_epsilon = 1e-05
scale_epsilon = 1e-06
code_limit = 15.0
adapter_scale = 2.0
rope_theta = 500000.0
rope_factor = 8.0
low_factor = 1.0
high_factor = 4.0
initial_context = 8192.0

NZ = 8
NY = 4
CHUNKS = 4
HALF = NZ // 2
STEPS = NZ - 1


def frequencies(positions):
    pair_index = jnp.arange(HEAD // 2, dtype=F32)
    inverse = jnp.exp(pair_index * (-2.0 * math.log(rope_theta) / HEAD))
    wavelength = 2.0 * math.pi / inverse
    blend = (initial_context / wavelength - low_factor) / (high_factor - low_factor)
    middle = (1.0 - blend) * inverse / rope_factor + blend * inverse
    adjusted = jnp.where(
        wavelength < initial_context / high_factor,
        inverse,
        jnp.where(wavelength > initial_context / low_factor, inverse / rope_factor, middle),
    )
    angles = positions.astype(F32)[:, None] * adjusted[None, :]
    return (jnp.cos(angles), jnp.sin(angles))


def prepare_kernel(steps, hidden_ref, gain_ref, base_ref, down_ref, up_ref, normed_ref, weight_ref, picked, squares):
    step = pl.program_id(0)
    tp = lax.axis_index("tp")
    width = hidden_ref.shape[1]
    values = hidden_ref[...].astype(F32)
    total = None
    for start in range(0, width, 128):
        part = values[:, start : start + 128]
        total = part * part if total is None else total + part * part

    @pl.when(step == 0)
    def _():
        squares[...] = total

    @pl.when(step > 0)
    def _():
        squares[...] += total

    mine = pl.ds(pl.multiple_of(tp * 128, 128), 128)
    picked[step] = hidden_ref[:, mine].astype(F32) * gain_ref[:, mine].astype(F32)

    low_rank = jnp.dot(
        down_ref[...] * adapter_scale, up_ref[...], preferred_element_type=F32
    )
    merged = base_ref[...].astype(F32) + low_rank
    by_column = jnp.max(jnp.abs(merged), axis=0, keepdims=True)
    stacked = jnp.concatenate(
        [by_column[:, start : start + BLOCK] for start in range(0, width, BLOCK)], axis=0
    )
    largest = jnp.max(stacked, axis=1, keepdims=True) + scale_epsilon
    largest = jnp.broadcast_to(largest, stacked.shape)
    scale = jnp.full(stacked.shape, 2.0**-23, F32)
    inverse = jnp.full(stacked.shape, 2.0**23, F32)
    for power in range(-23, 1):
        above = largest > code_limit * 2.0**power
        scale = jnp.where(above, 2.0 ** (power + 1), scale)
        inverse = jnp.where(above, 2.0 ** -(power + 1), inverse)
    for index, start in enumerate(range(0, width, BLOCK)):
        codes = jnp.floor(merged[:, start : start + BLOCK] * inverse[index : index + 1] + 0.5)
        weight_ref[:, start : start + BLOCK] = (codes * scale[index : index + 1]).astype(BF16)

    @pl.when(step == steps - 1)
    def _():
        mean_square = jnp.sum(squares[...], axis=1, keepdims=True) / (steps * width)
        factor = lax.rsqrt(mean_square + norm_epsilon)
        for group in range(steps):
            normed_ref[group * 128 : (group + 1) * 128, :] = (picked[group] * factor).astype(BF16)


def prepare(hidden, gain, base_rows, down, up, groups):
    rows, width = hidden.shape
    block = width // groups
    return pl.pallas_call(
        functools.partial(prepare_kernel, groups),
        grid=(groups,),
        in_specs=[
            pl.BlockSpec((rows, block), lambda i: (0, i)),
            pl.BlockSpec((1, block), lambda i: (0, i)),
            pl.BlockSpec((BLOCK, block), lambda i: (0, i)),
            pl.BlockSpec(down.shape, lambda i: (0, 0)),
            pl.BlockSpec((up.shape[0], block), lambda i: (0, i)),
        ],
        out_specs=[
            pl.BlockSpec((groups * rows, 128), lambda i: (0, 0)),
            pl.BlockSpec((BLOCK, block), lambda i: (0, i)),
        ],
        out_shape=[
            jax.ShapeDtypeStruct((groups * rows, 128), BF16),
            jax.ShapeDtypeStruct((BLOCK, width), BF16),
        ],
        scratch_shapes=[
            pltpu.VMEM((groups, rows, 128), F32),
            pltpu.VMEM((rows, 128), F32),
        ],
        compiler_params=pltpu.CompilerParams(dimension_semantics=("arbitrary",)),
    )(hidden, gain, base_rows, down, up)


def project_kernel(
    n_ref, w_ref, cos_ref, sin_ref, out_ref,
    acts, weights, sums, ring_z, ring_x, swap_x, swap_z,
    local_sem, n_send, n_recv, a_send, a_recv, b_send, b_recv, w_send, w_recv,
    rz_send, rz_recv, rx_send, rx_recv, sx_send, sx_recv, sz_send, sz_recv,
):
    f = lax.axis_index("fsdp")
    t = lax.axis_index("tp")
    z, x = f // 2, f % 2
    y, c = t // 2, t % 2
    peer_x = {"fsdp": z * 2 + (1 - x)}
    place = c * NY + y
    cols = weights.shape[1]
    cw = cols // CHUNKS
    qw = cw // 4

    def zmod(value):
        return (value + 2 * NZ) % NZ

    def remote(src, dst, send, recv, device):
        return pltpu.make_async_remote_copy(
            src_ref=src, dst_ref=dst, send_sem=send, recv_sem=recv,
            device_id=device, device_id_type=pl.DeviceIdType.MESH,
        )

    barrier = pltpu.get_barrier_semaphore()

    @pl.loop(1, 2 * NZ)
    def _(step):
        pl.semaphore_signal(
            barrier, inc=1, device_id={"fsdp": (f + step) % (2 * NZ)},
            device_id_type=pl.DeviceIdType.MESH,
        )

    @pl.loop(1, 2 * NY)
    def _(step):
        pl.semaphore_signal(
            barrier, inc=1, device_id={"tp": (t + step) % (2 * NY)},
            device_id_type=pl.DeviceIdType.MESH,
        )

    pl.semaphore_wait(barrier, 2 * NZ - 1 + 2 * NY - 1)

    def lane(index, size):
        return pl.ds(pl.multiple_of(index * size, size), size)

    my_lane = lane(place, 128)

    def n_copy(source, target):
        return remote(
            n_ref.at[lane(target, 128), :], acts.at[lane(source, 128), my_lane],
            n_send.at[target], n_recv.at[source], {"fsdp": target},
        )

    own_n = pltpu.make_async_copy(
        n_ref.at[lane(f, 128), :], acts.at[lane(f, 128), my_lane], local_sem.at[0]
    )
    own_n.start()

    @pl.loop(1, HALF + 1)
    def _(k):
        for flip in (0, 1):
            n_copy(f, zmod(z + k) * 2 + (x + flip) % 2).start()

            @pl.when(k < HALF)
            def _():
                n_copy(f, zmod(z - k) * 2 + (x + flip) % 2).start()

    n_copy(f, z * 2 + 1 - x).start()

    def w_copy(q, target, source):
        row = (source % 2) * NY + source // 2
        return remote(
            w_ref.at[:, pl.ds(pl.multiple_of(target * cols + q * cw, cw), cw)],
            weights.at[lane(row, BLOCK), lane(q, cw)],
            w_send.at[q, target], w_recv.at[q, source], {"tp": target},
        )

    def w_own(q):
        return pltpu.make_async_copy(
            w_ref.at[:, pl.ds(pl.multiple_of(t * cols + q * cw, cw), cw)],
            weights.at[lane(place, BLOCK), lane(q, cw)], local_sem.at[1 + q],
        )

    def w_start(q):
        for dy, dc in ((1, 0), (3, 0), (1, 1), (3, 1), (2, 0), (2, 1), (0, 1)):
            w_copy(q, ((y + dy) % NY) * 2 + (c + dc) % 2, t).start()
        w_own(q).start()

    w_start(0)

    def block_of(j, which):
        return zmod(z - (j + 1)) if which == 0 else zmod(z + (j + 1) % HALF)

    def a_copy(j, which, source_y, target_y):
        rows = lane(block_of(j, which), 256)
        view = acts.at[rows, lane(c * NY + source_y, 128)]
        return remote(
            view, view, a_send.at[2 * j + which, target_y], a_recv.at[2 * j + which, source_y],
            {"tp": target_y * 2 + c},
        )

    def b_copy(j, which, half):
        view = acts.at[lane(block_of(j, which), 256), lane(half, 128 * NY)]
        return remote(
            view, view, b_send.at[2 * j + which], b_recv.at[2 * j + which], {"tp": y * 2 + 1 - c}
        )

    def stage_a(j):
        for which in (0, 1):
            block = block_of(j, which)
            for other in (0, 1):
                source = block * 2 + other

                @pl.when(source != f)
                def _():
                    n_copy(source, f).wait_recv()

                @pl.when(source == f)
                def _():
                    own_n.wait()

            for dy in (1, 3, 2):
                a_copy(j, which, y, (y + dy) % NY).start()

    def stage_b(j):
        for which in (0, 1):
            for dy in (1, 3, 2):
                a_copy(j, which, (y + dy) % NY, y).wait_recv()
            b_copy(j, which, c).start()

    def stage_c(j):
        for which in (0, 1):
            b_copy(j, which, 1 - c).wait_recv()

    stage_a(0)
    stage_a(1)
    stage_b(0)

    def x_copy(q, j, which):
        rows = pl.ds(pl.multiple_of(block_of(j, which) * 256 + (1 - x) * 128, 128), 128)
        return remote(
            sums.at[rows, pl.ds(pl.multiple_of(q * cw + 2 * qw, qw), 2 * qw)],
            swap_x.at[q, 2 * j + which], sx_send.at[q, 2 * j + which],
            sx_recv.at[q, 2 * j + which], peer_x,
        )

    def products(q, j):
        for which in (0, 1):
            rows = lane(block_of(j, which), 256)
            value = jnp.dot(acts[rows, :], weights[:, lane(q, cw)], preferred_element_type=F32)
            sums[rows, lane(q, cw)] = value.astype(BF16)
            x_copy(q, j, which).start()

    def merge(q, j):
        for which in (0, 1):
            x_copy(q, j, which).wait_recv()
            rows = pl.ds(pl.multiple_of(block_of(j, which) * 256 + x * 128, 128), 128)
            here = pl.ds(pl.multiple_of(q * cw + 2 * qw, qw), 2 * qw)
            sums[rows, here] = (
                sums[rows, here].astype(F32) + swap_x[q, 2 * j + which].astype(F32)
            ).astype(BF16)

    def ring(kind, q, s, way):
        block = zmod(z - 1 - s) if way == 0 else zmod(z + 1 + s)
        target = zmod(z + 1) if way == 0 else zmod(z - 1)
        if kind == 0:
            rows = lane(block, 256)
        else:
            rows = pl.ds(pl.multiple_of(block * 256 + x * 128, 128), 128)
        here = pl.ds(pl.multiple_of(q * cw + (2 * kind + way) * qw, qw), qw)
        slots = ring_z if kind == 0 else ring_x
        sends = rz_send if kind == 0 else rx_send
        recvs = rz_recv if kind == 0 else rx_recv
        view = sums.at[rows, here]

        def hop(step):
            return remote(
                view, slots.at[q, way, step], sends.at[q, way, step], recvs.at[q, way, step],
                {"fsdp": target * 2 + x},
            )

        def arrived():
            hop(s - 1).wait_recv()
            return sums[rows, here].astype(F32) + slots[q, way, s - 1].astype(F32)

        return rows, here, hop, arrived

    def ring_early(kind, q, s):
        for way in (0, 1):
            rows, here, hop, arrived = ring(kind, q, s, way)

            @pl.when(s > 0)
            def _():
                sums[rows, here] = arrived().astype(BF16)

            hop(s).start()

    def finish(q, which, value):
        turned = value * cos_ref[...] + pltpu.roll(value, HEAD // 2, 1) * sin_ref[...]
        out_ref[:, pl.ds(pl.multiple_of(q * cw + which * qw, qw), qw)] = turned.astype(BF16)

    def z_copy(q):
        rows = pl.ds(pl.multiple_of(z * 256 + (1 - x) * 128, 128), 128)
        return remote(
            sums.at[rows, pl.ds(pl.multiple_of(q * cw, cw), 2 * qw)],
            swap_z.at[q], sz_send.at[q], sz_recv.at[q], peer_x,
        )

    def ring_late(kind, q, s):
        for way in (0, 1):
            rows, here, hop, arrived = ring(kind, q, s, way)
            value = arrived()

            @pl.when(s < STEPS)
            def _():
                sums[rows, here] = value.astype(BF16)
                hop(s).start()

            @pl.when(s == STEPS)
            def _():
                if kind == 0:
                    sums[rows, here] = value.astype(BF16)
                else:
                    finish(q, 2 + way, value)

        if kind == 0:

            @pl.when(s == STEPS)
            def _():
                z_copy(q).start()

    def last_z(q):
        z_copy(q).wait_recv()
        rows = pl.ds(pl.multiple_of(z * 256 + x * 128, 128), 128)
        for way in (0, 1):
            here = pl.ds(pl.multiple_of(q * cw + way * qw, qw), qw)
            value = sums[rows, here].astype(F32) + swap_z[q, :, way * qw : (way + 1) * qw].astype(
                F32
            )
            finish(q, way, value)

    @pl.loop(0, HALF * (CHUNKS + 1) + 1)
    def _(r):
        q, j = r // HALF, r % HALF

        @pl.when(r == 0)
        def _():
            stage_a(2)
            stage_b(1)

        @pl.when(r == 1)
        def _():
            stage_a(3)
            stage_b(2)

        @pl.when(r == 2)
        def _():
            stage_b(3)

        @pl.when((r > 0) & (r < CHUNKS))
        def _():
            w_start(r)

        @pl.when(r < HALF)
        def _():
            stage_c(j)

        @pl.when((q >= 2) & (j == 0))
        def _():
            last_z(q - 2)

        q1, j1 = (r + HALF - 1) // HALF - 1, (r + HALF - 1) % HALF

        @pl.when((r >= 1) & (q1 < CHUNKS))
        def _():
            merge(q1, j1)
            ring_early(1, q1, j1)

        @pl.when(q1 >= 1)
        def _():
            ring_late(1, q1 - 1, j1 + HALF)

        @pl.when((q < CHUNKS) & (j == 0))
        def _():
            w_own(q).wait()

            @pl.loop(1, 2 * NY)
            def _(step):
                w_copy(q, t, (t + step) % (2 * NY)).wait_recv()

        @pl.when(q < CHUNKS)
        def _():
            products(q, j)
            ring_early(0, q, j)

        @pl.when((q >= 1) & (q <= CHUNKS))
        def _():
            ring_late(0, q - 1, j + HALF)

    @pl.loop(1, 2 * NZ)
    def _(step):
        n_copy(f, (f + step) % (2 * NZ)).wait_send()

    @pl.loop(0, HALF)
    def _(j):
        for which in (0, 1):
            for dy in (1, 2, 3):
                a_copy(j, which, y, (y + dy) % NY).wait_send()
            b_copy(j, which, c).wait_send()

    @pl.loop(0, CHUNKS)
    def _(q):
        @pl.loop(1, 2 * NY)
        def _(step):
            w_copy(q, (t + step) % (2 * NY), t).wait_send()

        @pl.loop(0, HALF)
        def _(j):
            for which in (0, 1):
                x_copy(q, j, which).wait_send()

        @pl.loop(0, STEPS)
        def _(s):
            for kind in (0, 1):
                for way in (0, 1):
                    ring(kind, q, s, way)[2](s).wait_send()

        z_copy(q).wait_send()


def project(normed, weight, cosine, sine, groups, members):
    width = weight.shape[1]
    cols = width // members
    tokens = groups * 128
    cw = cols // CHUNKS
    qw = cw // 4
    dma = pltpu.SemaphoreType.DMA
    any_spec = pl.BlockSpec(memory_space=pl.ANY)
    vmem_spec = pl.BlockSpec(memory_space=pltpu.VMEM)
    return pl.pallas_call(
        project_kernel,
        in_specs=[any_spec, any_spec, vmem_spec, vmem_spec],
        out_specs=vmem_spec,
        out_shape=jax.ShapeDtypeStruct((128, cols), BF16),
        scratch_shapes=[
            pltpu.VMEM((tokens, members * BLOCK), BF16),
            pltpu.VMEM((members * BLOCK, cols), BF16),
            pltpu.VMEM((tokens, cols), BF16),
            pltpu.VMEM((CHUNKS, 2, STEPS, 256, qw), BF16),
            pltpu.VMEM((CHUNKS, 2, STEPS, 128, qw), BF16),
            pltpu.VMEM((CHUNKS, NZ, 128, 2 * qw), BF16),
            pltpu.VMEM((CHUNKS, 128, 2 * qw), BF16),
            dma((1 + CHUNKS,)),
            dma((groups,)), dma((groups,)),
            dma((NZ, NY)), dma((NZ, NY)),
            dma((NZ,)), dma((NZ,)),
            dma((CHUNKS, members)), dma((CHUNKS, members)),
            dma((CHUNKS, 2, STEPS)), dma((CHUNKS, 2, STEPS)),
            dma((CHUNKS, 2, STEPS)), dma((CHUNKS, 2, STEPS)),
            dma((CHUNKS, NZ)), dma((CHUNKS, NZ)),
            dma((CHUNKS,)), dma((CHUNKS,)),
        ],
        compiler_params=pltpu.CompilerParams(
            collective_id=0, has_side_effects=True, vmem_limit_bytes=48 * 1024 * 1024
        ),
    )(normed, weight, cosine, sine)


def solution(mesh):
    groups, members = mesh.shape["fsdp"], mesh.shape["tp"]

    def shards(hidden, base_weight, adapter_down, adapter_up, norm_gain, positions):
        normed, weight = prepare(
            hidden, norm_gain[None, :], base_weight, adapter_down, adapter_up, groups
        )
        cosine, sine = frequencies(positions)
        return project(
            normed, weight,
            jnp.concatenate([cosine, cosine], axis=1),
            jnp.concatenate([-sine, sine], axis=1),
            groups, members,
        )

    placed = (
        P(("rep", "fsdp"), None),
        P(("rep", "fsdp", "tp"), None),
        P(("rep", "fsdp", "tp"), None),
        P("rep", None),
        P("rep"),
        P(("rep", "fsdp")),
    )
    return jax.shard_map(
        shards, mesh=mesh, in_specs=placed, out_specs=P(("rep", "fsdp"), "tp"), check_vma=False
    )
```

```python
import functools
import math

import jax
import jax.numpy as jnp
from jax import lax
from jax.experimental import pallas as pl
from jax.experimental.pallas import tpu as pltpu
from jax.sharding import PartitionSpec as P

HEAD = 128
BLOCK = 128
F32 = jnp.float32
BF16 = jnp.bfloat16

norm_epsilon = 1e-05
scale_epsilon = 1e-06
code_limit = 15.0
adapter_scale = 2.0
rope_theta = 500000.0
rope_factor = 8.0
low_factor = 1.0
high_factor = 4.0
initial_context = 8192.0

NZ = 8
NY = 4
CHUNKS = 8
STRIDE = 2
LAST = NZ // 2
OFFSETS = (4, 3, -3, 2, -2, 1, -1, 0)
STEP_BLOCKS = ((0,), (1, 2), (3, 4), (5, 6), (7,))


def frequencies(positions):
    pair_index = jnp.arange(HEAD // 2, dtype=F32)
    inverse = jnp.exp(pair_index * (-2.0 * math.log(rope_theta) / HEAD))
    wavelength = 2.0 * math.pi / inverse
    blend = (initial_context / wavelength - low_factor) / (high_factor - low_factor)
    middle = (1.0 - blend) * inverse / rope_factor + blend * inverse
    adjusted = jnp.where(
        wavelength < initial_context / high_factor,
        inverse,
        jnp.where(wavelength > initial_context / low_factor, inverse / rope_factor, middle),
    )
    angles = positions.astype(F32)[:, None] * adjusted[None, :]
    return (jnp.cos(angles), jnp.sin(angles))


def project_kernel(
    hidden_hbm, base_hbm, gain_ref, down_ref, up_ref, cos_ref, sin_ref, out_ref,
    hidden, base, normed, coded, acts, weights, sums, ring_z, ring_x, swap_x, swap_z,
    load_sem, local_sem, n_send, n_recv, a_send, a_recv, h_send, h_recv, b_send, b_recv,
    w_send, w_recv, rz_send, rz_recv, rx_send, rx_recv, sx_send, sx_recv, sz_send, sz_recv,
):
    f = lax.axis_index("fsdp")
    t = lax.axis_index("tp")
    z, x = f // 2, f % 2
    y, c = t // 2, t % 2
    peer_x = {"fsdp": z * 2 + (1 - x)}
    place = c * NY + y
    cols = weights.shape[1]
    cw = cols // CHUNKS
    tile = cw // 2
    groups = 2 * NZ
    width = hidden.shape[1]

    load_hidden = pltpu.make_async_copy(hidden_hbm, hidden, load_sem.at[0])
    load_base = pltpu.make_async_copy(base_hbm, base, load_sem.at[1])
    load_hidden.start()
    load_base.start()

    def zmod(value):
        return (value + NZ) % NZ

    def remote(src, dst, send, recv, device):
        return pltpu.make_async_remote_copy(
            src_ref=src, dst_ref=dst, send_sem=send, recv_sem=recv,
            device_id=device, device_id_type=pl.DeviceIdType.MESH,
        )

    def lane(index, size):
        return pl.ds(pl.multiple_of(index * size, size), size)

    barrier = pltpu.get_barrier_semaphore()

    @pl.loop(1, groups)
    def _(step):
        pl.semaphore_signal(
            barrier, inc=1, device_id={"fsdp": (f + step) % groups},
            device_id_type=pl.DeviceIdType.MESH,
        )

    @pl.loop(1, 2 * NY)
    def _(step):
        pl.semaphore_signal(
            barrier, inc=1, device_id={"tp": (t + step) % (2 * NY)},
            device_id_type=pl.DeviceIdType.MESH,
        )

    load_hidden.wait()
    span = width // groups

    def squares(group, total):
        values = hidden[:, lane(group, span)].astype(F32)
        for start in range(0, span, 128):
            part = values[:, start : start + 128]
            total = total + part * part
        return total

    total = lax.fori_loop(0, groups, squares, jnp.zeros((128, 128), F32))
    mean_square = jnp.sum(total, axis=1, keepdims=True) / width
    factor = jnp.broadcast_to(lax.rsqrt(mean_square + norm_epsilon), (128, 128))

    @pl.loop(0, groups)
    def _(group):
        mine = lane(group * (span // 128) + t, 128)
        normed[lane(group, 128), :] = (
            hidden[:, mine].astype(F32) * factor * gain_ref[:, mine].astype(F32)
        ).astype(BF16)

    pl.semaphore_wait(barrier, groups - 1 + 2 * NY - 1)

    def n_copy(source, target):
        return remote(
            normed.at[lane(target, 128), :], acts.at[lane(source, 128), lane(place, 128)],
            n_send.at[target], n_recv.at[source], {"fsdp": target},
        )

    own_n = pltpu.make_async_copy(
        normed.at[lane(f, 128), :], acts.at[lane(f, 128), lane(place, 128)], local_sem.at[0]
    )
    for offset in OFFSETS[:-1]:
        for flip in (0, 1):
            n_copy(f, zmod(z - offset) * 2 + (x + flip) % 2).start()
    n_copy(f, z * 2 + 1 - x).start()
    own_n.start()

    def w_copy(q, target, source):
        row = (source % 2) * NY + source // 2
        return remote(
            coded.at[:, pl.ds(pl.multiple_of(target * cols + q * cw, cw), cw)],
            weights.at[lane(row, BLOCK), lane(q, cw)],
            w_send.at[q, target], w_recv.at[q, source], {"tp": target},
        )

    def w_own(q):
        return pltpu.make_async_copy(
            coded.at[:, pl.ds(pl.multiple_of(t * cols + q * cw, cw), cw)],
            weights.at[lane(place, BLOCK), lane(q, cw)], local_sem.at[1 + q],
        )

    def w_start(q):
        @pl.loop(0, 2 * NY)
        def _(target):
            here = pl.ds(pl.multiple_of(target * cols + q * cw, cw), cw)
            low_rank = lax.dot_general(
                down_ref[...] * adapter_scale, up_ref[:, here], (((0,), (0,)), ((), ())),
                preferred_element_type=F32,
            )
            merged = base[:, here].astype(F32) + low_rank
            by_column = jnp.max(jnp.abs(merged), axis=0, keepdims=True)
            stacked = jnp.concatenate(
                [by_column[:, start : start + BLOCK] for start in range(0, cw, BLOCK)], axis=0
            )
            largest = jnp.max(stacked, axis=1, keepdims=True) + scale_epsilon
            largest = jnp.broadcast_to(largest, stacked.shape)
            scale = jnp.full(stacked.shape, 2.0**-23, F32)
            inverse = jnp.full(stacked.shape, 2.0**23, F32)
            for power in range(-23, 1):
                above = largest > code_limit * 2.0**power
                scale = jnp.where(above, 2.0 ** (power + 1), scale)
                inverse = jnp.where(above, 2.0 ** -(power + 1), inverse)
            result = []
            for index, start in enumerate(range(0, cw, BLOCK)):
                codes = jnp.floor(
                    merged[:, start : start + BLOCK] * inverse[index : index + 1] + 0.5
                )
                result.append((codes * scale[index : index + 1]).astype(BF16))
            coded[:, here] = jnp.concatenate(result, axis=1)

        for dy, dc in ((1, 0), (3, 0), (1, 1), (3, 1), (2, 0), (2, 1), (0, 1)):
            w_copy(q, ((y + dy) % NY) * 2 + (c + dc) % 2, t).start()
        w_own(q).start()

    def rows_of(i):
        return lane(zmod(z + OFFSETS[i]), 256)

    def a_copy(i, source_y, way):
        view = acts.at[rows_of(i), lane(c * NY + source_y, 128)]
        target = (y + (1 if way == 0 else NY - 1)) % NY
        return remote(view, view, a_send.at[i, way], a_recv.at[i, way], {"tp": target * 2 + c})

    def h_copy(i, source_y, way):
        rows = pl.ds(pl.multiple_of(zmod(z + OFFSETS[i]) * 256 + way * 128, 128), 128)
        view = acts.at[rows, lane(c * NY + source_y, 128)]
        target = (y + (1 if way == 0 else NY - 1)) % NY
        return remote(view, view, h_send.at[i, way], h_recv.at[i, way], {"tp": target * 2 + c})

    def b_copy(i, half):
        view = acts.at[rows_of(i), lane(half, 128 * NY)]
        return remote(view, view, b_send.at[i], b_recv.at[i], {"tp": y * 2 + 1 - c})

    down_y, up_y, far_y = (y + NY - 1) % NY, (y + 1) % NY, (y + 2) % NY

    def stage_a(i):
        block = zmod(z + OFFSETS[i])
        if OFFSETS[i]:
            for other in (0, 1):
                n_copy(block * 2 + other, f).wait_recv()
        else:
            n_copy(z * 2 + 1 - x, f).wait_recv()
            own_n.wait()
        for way in (0, 1):
            a_copy(i, y, way).start()

    def stage_h(i):
        for way, source in ((0, down_y), (1, up_y)):
            a_copy(i, source, way).wait_recv()
            h_copy(i, source, way).start()

    def stage_b(i):
        for way in (0, 1):
            h_copy(i, far_y, way).wait_recv()
        b_copy(i, c).start()

    def stage_c(i):
        b_copy(i, 1 - c).wait_recv()

    def x_copy(q, i):
        rows = pl.ds(pl.multiple_of(zmod(z + OFFSETS[i]) * 256 + (1 - x) * 128, 128), 128)
        here = pl.ds(pl.multiple_of(q * cw + tile, tile), tile)
        return remote(
            sums.at[rows, here], swap_x.at[q, i], sx_send.at[q, i], sx_recv.at[q, i], peer_x
        )

    def products(q, s):
        for i in STEP_BLOCKS[s]:
            value = jnp.dot(
                acts[rows_of(i), :], weights[:, lane(q, cw)], preferred_element_type=F32
            )
            sums[rows_of(i), lane(q, cw)] = value.astype(BF16)
            x_copy(q, i).start()

    def finish(q, which, value):
        turned = value * cos_ref[...] + pltpu.roll(value, HEAD // 2, 1) * sin_ref[...]
        out_ref[:, pl.ds(pl.multiple_of(q * cw + which * tile, tile), tile)] = turned.astype(BF16)

    def z_copy(q):
        rows = pl.ds(pl.multiple_of(z * 256 + (1 - x) * 128, 128), 128)
        return remote(
            sums.at[rows, pl.ds(pl.multiple_of(q * cw, cw), tile)],
            swap_z.at[q], sz_send.at[q], sz_recv.at[q], peer_x,
        )

    def ring(kind, q, s, way):
        size = 256 if kind == 0 else 128
        block = zmod(z + (LAST - s)) if way == 0 else zmod(z - (LAST - s))
        first = block * 256 if kind == 0 else block * 256 + x * 128
        here = pl.ds(pl.multiple_of(q * cw + kind * tile, tile), tile)
        slots, sends, recvs = (
            (ring_z, rz_send, rz_recv) if kind == 0 else (ring_x, rx_send, rx_recv)
        )
        target = zmod(z + 1) if way == 0 else zmod(z - 1)

        def hop(step):
            if step == 0:
                half = size // 2
                src = sums.at[pl.ds(pl.multiple_of(first + way * half, half), half), here]
                dst = slots.at[q, way, 0, pl.ds(0, half)]
            else:
                src = sums.at[pl.ds(pl.multiple_of(first, size), size), here]
                dst = slots.at[q, way, step]
            return remote(
                src, dst, sends.at[q, way, step], recvs.at[q, way, step],
                {"fsdp": target * 2 + x},
            )

        return size, first, here, slots, hop

    def ring_step(kind, q, s):
        size, first, here, slots, hop = ring(kind, q, s, 0)
        half = size // 2

        def read(start, count):
            rows = pl.ds(pl.multiple_of(start, count), count)
            return sums[rows, here].astype(F32)

        def put(start, count, value):
            sums[pl.ds(pl.multiple_of(start, count), count), here] = value.astype(BF16)

        def swapped(i, start=0, count=size):
            return swap_x[q, i, start : start + count].astype(F32)

        if kind == 1:
            for i in STEP_BLOCKS[s]:
                x_copy(q, i).wait_recv()
        if s == 0:
            if kind == 1:
                put(first, size, read(first, size) + swapped(0))
            for way in (0, 1):
                ring(kind, q, s, way)[4](0).start()
        elif s < LAST:
            for way in (0, 1):
                size, first, here, slots, hop = ring(kind, q, s, way)
                i = STEP_BLOCKS[s][way]
                hop(s - 1).wait_recv()
                if s == 1:
                    near = first + way * half
                    value = read(near, half) + slots[q, way, 0, 0:half].astype(F32)
                    if kind == 1:
                        value = value + swapped(i, way * half, half)
                        other = first + (1 - way) * half
                        put(other, half, read(other, half) + swapped(i, (1 - way) * half, half))
                    put(near, half, value)
                else:
                    value = read(first, size) + slots[q, way, s - 1].astype(F32)
                    if kind == 1:
                        value = value + swapped(i)
                    put(first, size, value)
                hop(s).start()
        else:
            value = read(first, size)
            if kind == 1:
                value = value + swapped(7)
            for way in (0, 1):
                ring(kind, q, s, way)[4](s - 1).wait_recv()
                value = value + slots[q, way, s - 1].astype(F32)
            if kind == 0:
                put(first, size, value)
                z_copy(q).start()
            else:
                finish(q, 1, value)

    def last_z(q):
        z_copy(q).wait_recv()
        rows = pl.ds(pl.multiple_of(z * 256 + x * 128, 128), 128)
        here = pl.ds(pl.multiple_of(q * cw, cw), tile)
        finish(q, 0, sums[rows, here].astype(F32) + swap_z[q].astype(F32))

    load_base.wait()
    w_start(0)
    stage_a(0)
    w_start(1)
    stage_a(1), stage_a(2), stage_h(0)
    stage_a(3), stage_a(4), stage_h(1), stage_h(2), stage_b(0)
    stage_a(5), stage_a(6), stage_h(3), stage_h(4), stage_b(1), stage_b(2)
    stage_a(7), stage_h(5), stage_h(6), stage_b(3), stage_b(4)
    stage_h(7), stage_b(5), stage_b(6)

    def at_chunk(start, run):
        @pl.when((start >= 0) & (start % STRIDE == 0) & (start < STRIDE * CHUNKS))
        def _():
            run(start // STRIDE)

    @pl.loop(0, STRIDE * (CHUNKS - 1) + LAST + 3)
    def _(r):
        at_chunk(r - LAST - 2, last_z)
        for s in range(LAST, -1, -1):
            at_chunk(r - s - 1, functools.partial(ring_step, 0, s=s))
            at_chunk(r - s - 2, functools.partial(ring_step, 1, s=s))

        @pl.when(r == 0)
        def _():
            stage_b(7)

        @pl.when(r + 2 < CHUNKS)
        def _():
            w_start(r + 2)

        for s in range(LAST + 1):

            @pl.when(r == s)
            def _():
                for i in STEP_BLOCKS[s]:
                    stage_c(i)

        def arrive(q):
            w_own(q).wait()

            @pl.loop(1, 2 * NY)
            def _(step):
                w_copy(q, t, (t + step) % (2 * NY)).wait_recv()

        at_chunk(r, arrive)
        for s in range(LAST, -1, -1):
            at_chunk(r - s, functools.partial(products, s=s))

    @pl.loop(1, groups)
    def _(step):
        n_copy(f, (f + step) % groups).wait_send()

    for i in range(NZ):
        for way in (0, 1):
            a_copy(i, y, way).wait_send()
            h_copy(i, y, way).wait_send()
        b_copy(i, c).wait_send()

    @pl.loop(0, CHUNKS)
    def _(q):
        @pl.loop(1, 2 * NY)
        def _(step):
            w_copy(q, (t + step) % (2 * NY), t).wait_send()

        for i in range(NZ):
            x_copy(q, i).wait_send()
        for kind in (0, 1):
            for way in (0, 1):
                for s in range(LAST):
                    ring(kind, q, s, way)[4](s).wait_send()
        z_copy(q).wait_send()


def project(hidden, base, gain, down, up, cosine, sine, groups, members):
    width = base.shape[1]
    cols = width // members
    tokens = groups * 128
    tile = cols // CHUNKS // 2
    dma = pltpu.SemaphoreType.DMA
    any_spec = pl.BlockSpec(memory_space=pl.ANY)
    vmem_spec = pl.BlockSpec(memory_space=pltpu.VMEM)
    pair = lambda *shape: [dma(shape), dma(shape)]
    return pl.pallas_call(
        project_kernel,
        in_specs=[any_spec, any_spec] + [vmem_spec] * 5,
        out_specs=vmem_spec,
        out_shape=jax.ShapeDtypeStruct((128, cols), BF16),
        scratch_shapes=[
            pltpu.VMEM((128, width), BF16),
            pltpu.VMEM((128, width), BF16),
            pltpu.VMEM((tokens, 128), BF16),
            pltpu.VMEM((128, width), BF16),
            pltpu.VMEM((tokens, members * BLOCK), BF16),
            pltpu.VMEM((members * BLOCK, cols), BF16),
            pltpu.VMEM((tokens, cols), BF16),
            pltpu.VMEM((CHUNKS, 2, LAST, 256, tile), BF16),
            pltpu.VMEM((CHUNKS, 2, LAST, 128, tile), BF16),
            pltpu.VMEM((CHUNKS, NZ, 128, tile), BF16),
            pltpu.VMEM((CHUNKS, 128, tile), BF16),
            dma((2,)),
            dma((1 + CHUNKS,)),
            *pair(groups),
            *pair(NZ, 2),
            *pair(NZ, 2),
            *pair(NZ),
            *pair(CHUNKS, members),
            *pair(CHUNKS, 2, LAST),
            *pair(CHUNKS, 2, LAST),
            *pair(CHUNKS, NZ),
            *pair(CHUNKS),
        ],
        compiler_params=pltpu.CompilerParams(
            collective_id=0, has_side_effects=True, vmem_limit_bytes=60 * 1024 * 1024
        ),
    )(hidden, base, gain, down, up, cosine, sine)


def solution(mesh):
    groups, members = mesh.shape["fsdp"], mesh.shape["tp"]

    def shards(hidden, base_weight, adapter_down, adapter_up, norm_gain, positions):
        cosine, sine = frequencies(positions)
        return project(
            hidden, base_weight, norm_gain[None, :], adapter_down.T, adapter_up,
            jnp.concatenate([cosine, cosine], axis=1),
            jnp.concatenate([-sine, sine], axis=1),
            groups, members,
        )

    placed = (
        P(("rep", "fsdp"), None),
        P(("rep", "fsdp", "tp"), None),
        P(("rep", "fsdp", "tp"), None),
        P("rep", None),
        P("rep"),
        P(("rep", "fsdp")),
    )
    return jax.shard_map(
        shards, mesh=mesh, in_specs=placed, out_specs=P(("rep", "fsdp"), "tp"), check_vma=False
    )
```

```python
import functools
import math

import jax
import jax.numpy as jnp
from jax import lax
from jax.experimental import pallas as pl
from jax.experimental.pallas import tpu as pltpu
from jax.sharding import PartitionSpec as P

HEAD = 128
BLOCK = 128
F32 = jnp.float32
BF16 = jnp.bfloat16

norm_epsilon = 1e-05
scale_epsilon = 1e-06
code_limit = 15.0
adapter_scale = 2.0
rope_theta = 500000.0
rope_factor = 8.0
low_factor = 1.0
high_factor = 4.0
initial_context = 8192.0

NZ = 8
NY = 4
CHUNKS = 8
STRIDE = 1
LAST = NZ // 2
OFFSETS = (4, 3, -3, 2, -2, 1, -1, 0)
STEP_BLOCKS = ((0,), (1, 2), (3, 4), (5, 6), (7,))


def frequencies(positions):
    pair_index = jnp.arange(HEAD // 2, dtype=F32)
    inverse = jnp.exp(pair_index * (-2.0 * math.log(rope_theta) / HEAD))
    wavelength = 2.0 * math.pi / inverse
    blend = (initial_context / wavelength - low_factor) / (high_factor - low_factor)
    middle = (1.0 - blend) * inverse / rope_factor + blend * inverse
    adjusted = jnp.where(
        wavelength < initial_context / high_factor,
        inverse,
        jnp.where(wavelength > initial_context / low_factor, inverse / rope_factor, middle),
    )
    angles = positions.astype(F32)[:, None] * adjusted[None, :]
    return (jnp.cos(angles), jnp.sin(angles))


def project_kernel(
    hidden_hbm, base_hbm, gain_ref, down_ref, up_ref, cos_ref, sin_ref, out_ref,
    hidden, base, normed, coded, acts, weights, sums, ring_z, ring_x, swap_x, swap_z,
    load_sem, local_sem, n_send, n_recv, a_send, a_recv, h_send, h_recv, b_send, b_recv,
    w_send, w_recv, rz_send, rz_recv, rx_send, rx_recv, sx_send, sx_recv, sz_send, sz_recv,
):
    f = lax.axis_index("fsdp")
    t = lax.axis_index("tp")
    z, x = f // 2, f % 2
    y, c = t // 2, t % 2
    peer_x = {"fsdp": z * 2 + (1 - x)}
    place = c * NY + y
    cols = weights.shape[1]
    cw = cols // CHUNKS
    tile = cw // 2
    groups = 2 * NZ
    width = hidden.shape[1]

    load_hidden = pltpu.make_async_copy(hidden_hbm, hidden, load_sem.at[0])
    load_base = pltpu.make_async_copy(base_hbm, base, load_sem.at[1])
    load_hidden.start()
    load_base.start()

    def zmod(value):
        return (value + NZ) % NZ

    def remote(src, dst, send, recv, device):
        return pltpu.make_async_remote_copy(
            src_ref=src, dst_ref=dst, send_sem=send, recv_sem=recv,
            device_id=device, device_id_type=pl.DeviceIdType.MESH,
        )

    def lane(index, size):
        return pl.ds(pl.multiple_of(index * size, size), size)

    barrier = pltpu.get_barrier_semaphore()

    @pl.loop(1, groups)
    def _(step):
        pl.semaphore_signal(
            barrier, inc=1, device_id={"fsdp": (f + step) % groups},
            device_id_type=pl.DeviceIdType.MESH,
        )

    @pl.loop(1, 2 * NY)
    def _(step):
        pl.semaphore_signal(
            barrier, inc=1, device_id={"tp": (t + step) % (2 * NY)},
            device_id_type=pl.DeviceIdType.MESH,
        )

    load_hidden.wait()
    span = width // groups

    def squares(group, total):
        values = hidden[:, lane(group, span)].astype(F32)
        for start in range(0, span, 128):
            part = values[:, start : start + 128]
            total = total + part * part
        return total

    total = lax.fori_loop(0, groups, squares, jnp.zeros((128, 128), F32))
    mean_square = jnp.sum(total, axis=1, keepdims=True) / width
    members = 2 * NY
    chosen = lax.broadcasted_iota(jnp.int32, (members, 128), 0) == t
    factor = jnp.broadcast_to(lax.rsqrt(mean_square + norm_epsilon), (128, 128))

    @pl.loop(0, groups)
    def _(group):
        mine = lane(group * members + t, 128)
        gains = gain_ref[lane(group, members), :].astype(F32)
        gain = jnp.sum(jnp.where(chosen, gains, 0.0), axis=0, keepdims=True)
        normed[lane(group, 128), :] = (hidden[:, mine].astype(F32) * factor * gain).astype(BF16)

    pl.semaphore_wait(barrier, groups - 1 + 2 * NY - 1)

    def n_copy(source, target):
        return remote(
            normed.at[lane(target, 128), :], acts.at[lane(source, 128), lane(place, 128)],
            n_send.at[target], n_recv.at[source], {"fsdp": target},
        )

    own_n = pltpu.make_async_copy(
        normed.at[lane(f, 128), :], acts.at[lane(f, 128), lane(place, 128)], local_sem.at[0]
    )
    for offset in OFFSETS[:-1]:
        for flip in (0, 1):
            n_copy(f, zmod(z - offset) * 2 + (x + flip) % 2).start()
    n_copy(f, z * 2 + 1 - x).start()
    own_n.start()

    def w_copy(q, target, source):
        row = (source % 2) * NY + source // 2
        return remote(
            coded.at[:, pl.ds(pl.multiple_of(target * cols + q * cw, cw), cw)],
            weights.at[lane(row, BLOCK), lane(q, cw)],
            w_send.at[q, target], w_recv.at[q, source], {"tp": target},
        )

    def w_own(q):
        return pltpu.make_async_copy(
            coded.at[:, pl.ds(pl.multiple_of(t * cols + q * cw, cw), cw)],
            weights.at[lane(place, BLOCK), lane(q, cw)], local_sem.at[1 + q],
        )

    def w_start(q):
        doubled = down_ref[...] * adapter_scale
        views, merged, maxima = [], [], []
        for target in range(2 * NY):
            here = pl.ds(pl.multiple_of(target * cols + q * cw, cw), cw)
            low_rank = lax.dot_general(
                doubled, up_ref[:, here], (((0,), (0,)), ((), ())), preferred_element_type=F32
            )
            value = base[:, here].astype(F32) + low_rank
            by_column = jnp.max(jnp.abs(value), axis=0, keepdims=True)
            views.append(here)
            merged.append(value)
            maxima += [by_column[:, start : start + BLOCK] for start in range(0, cw, BLOCK)]
        stacked = jnp.concatenate(maxima, axis=0)
        largest = jnp.max(stacked, axis=1, keepdims=True) + scale_epsilon
        largest = jnp.broadcast_to(largest, stacked.shape)
        scale = jnp.full(stacked.shape, 2.0**-23, F32)
        inverse = jnp.full(stacked.shape, 2.0**23, F32)
        for power in range(-23, 1):
            above = largest > code_limit * 2.0**power
            scale = jnp.where(above, 2.0 ** (power + 1), scale)
            inverse = jnp.where(above, 2.0 ** -(power + 1), inverse)
        for target in range(2 * NY):
            result = []
            for part in range(cw // BLOCK):
                row = target * (cw // BLOCK) + part
                block = merged[target][:, part * BLOCK : (part + 1) * BLOCK]
                codes = jnp.floor(block * inverse[row : row + 1] + 0.5)
                result.append((codes * scale[row : row + 1]).astype(BF16))
            coded[:, views[target]] = jnp.concatenate(result, axis=1)

        for dy, dc in ((1, 0), (3, 0), (1, 1), (3, 1), (2, 0), (2, 1), (0, 1)):
            w_copy(q, ((y + dy) % NY) * 2 + (c + dc) % 2, t).start()
        w_own(q).start()

    def rows_of(i):
        return lane(zmod(z + OFFSETS[i]), 256)

    def a_copy(i, source_y, way):
        view = acts.at[rows_of(i), lane(c * NY + source_y, 128)]
        target = (y + (1 if way == 0 else NY - 1)) % NY
        return remote(view, view, a_send.at[i, way], a_recv.at[i, way], {"tp": target * 2 + c})

    def h_copy(i, source_y, way):
        rows = pl.ds(pl.multiple_of(zmod(z + OFFSETS[i]) * 256 + way * 128, 128), 128)
        view = acts.at[rows, lane(c * NY + source_y, 128)]
        target = (y + (1 if way == 0 else NY - 1)) % NY
        return remote(view, view, h_send.at[i, way], h_recv.at[i, way], {"tp": target * 2 + c})

    def b_copy(i, half):
        view = acts.at[rows_of(i), lane(half, 128 * NY)]
        return remote(view, view, b_send.at[i], b_recv.at[i], {"tp": y * 2 + 1 - c})

    down_y, up_y, far_y = (y + NY - 1) % NY, (y + 1) % NY, (y + 2) % NY

    def stage_a(i):
        block = zmod(z + OFFSETS[i])
        if OFFSETS[i]:
            for other in (0, 1):
                n_copy(block * 2 + other, f).wait_recv()
        else:
            n_copy(z * 2 + 1 - x, f).wait_recv()
            own_n.wait()
        for way in (0, 1):
            a_copy(i, y, way).start()

    def stage_h(i):
        for way, source in ((0, down_y), (1, up_y)):
            a_copy(i, source, way).wait_recv()
            h_copy(i, source, way).start()

    def stage_b(i):
        for way in (0, 1):
            h_copy(i, far_y, way).wait_recv()
        b_copy(i, c).start()

    def stage_c(i):
        b_copy(i, 1 - c).wait_recv()

    def x_copy(q, i):
        rows = pl.ds(pl.multiple_of(zmod(z + OFFSETS[i]) * 256 + (1 - x) * 128, 128), 128)
        here = pl.ds(pl.multiple_of(q * cw + tile, tile), tile)
        return remote(
            sums.at[rows, here], swap_x.at[q, i], sx_send.at[q, i], sx_recv.at[q, i], peer_x
        )

    def products(q, s):
        for i in STEP_BLOCKS[s]:
            value = jnp.dot(
                acts[rows_of(i), :], weights[:, lane(q, cw)], preferred_element_type=F32
            )
            sums[rows_of(i), lane(q, cw)] = value.astype(BF16)
            x_copy(q, i).start()

    def finish(q, which, value):
        turned = value * cos_ref[...] + pltpu.roll(value, HEAD // 2, 1) * sin_ref[...]
        out_ref[:, pl.ds(pl.multiple_of(q * cw + which * tile, tile), tile)] = turned.astype(BF16)

    def z_copy(q):
        rows = pl.ds(pl.multiple_of(z * 256 + (1 - x) * 128, 128), 128)
        return remote(
            sums.at[rows, pl.ds(pl.multiple_of(q * cw, cw), tile)],
            swap_z.at[q], sz_send.at[q], sz_recv.at[q], peer_x,
        )

    def ring(kind, q, s, way):
        size = 256 if kind == 0 else 128
        block = zmod(z + (LAST - s)) if way == 0 else zmod(z - (LAST - s))
        first = block * 256 if kind == 0 else block * 256 + x * 128
        here = pl.ds(pl.multiple_of(q * cw + kind * tile, tile), tile)
        slots, sends, recvs = (
            (ring_z, rz_send, rz_recv) if kind == 0 else (ring_x, rx_send, rx_recv)
        )
        target = zmod(z + 1) if way == 0 else zmod(z - 1)

        def hop(step):
            if step == 0:
                half = size // 2
                src = sums.at[pl.ds(pl.multiple_of(first + way * half, half), half), here]
                dst = slots.at[q, way, 0, pl.ds(0, half)]
            else:
                src = sums.at[pl.ds(pl.multiple_of(first, size), size), here]
                dst = slots.at[q, way, step]
            return remote(
                src, dst, sends.at[q, way, step], recvs.at[q, way, step],
                {"fsdp": target * 2 + x},
            )

        return size, first, here, slots, hop

    def ring_step(kind, q, s):
        size, first, here, slots, hop = ring(kind, q, s, 0)
        half = size // 2

        def read(start, count):
            rows = pl.ds(pl.multiple_of(start, count), count)
            return sums[rows, here].astype(F32)

        def put(start, count, value):
            sums[pl.ds(pl.multiple_of(start, count), count), here] = value.astype(BF16)

        def swapped(i, start=0, count=size):
            return swap_x[q, i, start : start + count].astype(F32)

        if kind == 1:
            for i in STEP_BLOCKS[s]:
                x_copy(q, i).wait_recv()
        if s == 0:
            if kind == 1:
                put(first, size, read(first, size) + swapped(0))
            for way in (0, 1):
                ring(kind, q, s, way)[4](0).start()
        elif s < LAST:
            for way in (0, 1):
                size, first, here, slots, hop = ring(kind, q, s, way)
                i = STEP_BLOCKS[s][way]
                hop(s - 1).wait_recv()
                if s == 1:
                    near = first + way * half
                    value = read(near, half) + slots[q, way, 0, 0:half].astype(F32)
                    if kind == 1:
                        value = value + swapped(i, way * half, half)
                        other = first + (1 - way) * half
                        put(other, half, read(other, half) + swapped(i, (1 - way) * half, half))
                    put(near, half, value)
                else:
                    value = read(first, size) + slots[q, way, s - 1].astype(F32)
                    if kind == 1:
                        value = value + swapped(i)
                    put(first, size, value)
                hop(s).start()
        else:
            value = read(first, size)
            if kind == 1:
                value = value + swapped(7)
            for way in (0, 1):
                ring(kind, q, s, way)[4](s - 1).wait_recv()
                value = value + slots[q, way, s - 1].astype(F32)
            if kind == 0:
                put(first, size, value)
                z_copy(q).start()
            else:
                finish(q, 1, value)

    def last_z(q):
        z_copy(q).wait_recv()
        rows = pl.ds(pl.multiple_of(z * 256 + x * 128, 128), 128)
        here = pl.ds(pl.multiple_of(q * cw, cw), tile)
        finish(q, 0, sums[rows, here].astype(F32) + swap_z[q].astype(F32))

    load_base.wait()
    w_start(0)
    stage_a(0)
    w_start(1)
    stage_a(1), stage_a(2), stage_h(0)
    stage_a(3), stage_a(4), stage_h(1), stage_h(2), stage_b(0)
    stage_a(5), stage_a(6), stage_h(3), stage_h(4), stage_b(1), stage_b(2)
    stage_a(7), stage_h(5), stage_h(6), stage_b(3), stage_b(4)
    stage_h(7)
    w_start(2), w_start(3)
    stage_b(5), stage_b(6)

    def at_chunk(start, run):
        @pl.when((start >= 0) & (start % STRIDE == 0) & (start < STRIDE * CHUNKS))
        def _():
            run(start // STRIDE)

    @pl.loop(0, STRIDE * (CHUNKS - 1) + LAST + 3)
    def _(r):
        at_chunk(r - LAST - 2, last_z)
        for s in range(LAST, -1, -1):
            at_chunk(r - s - 1, functools.partial(ring_step, 0, s=s))
            at_chunk(r - s - 2, functools.partial(ring_step, 1, s=s))

        @pl.when(r + 4 < CHUNKS)
        def _():
            w_start(r + 4)

        for s in range(LAST + 1):

            @pl.when(r == s)
            def _():
                for i in STEP_BLOCKS[s]:
                    stage_c(i)

        def arrive(q):
            w_own(q).wait()

            @pl.loop(1, 2 * NY)
            def _(step):
                w_copy(q, t, (t + step) % (2 * NY)).wait_recv()

        at_chunk(r, arrive)
        for s in range(LAST, -1, -1):
            at_chunk(r - s, functools.partial(products, s=s))

        @pl.when(r == 0)
        def _():
            stage_b(7)

    @pl.loop(1, groups)
    def _(step):
        n_copy(f, (f + step) % groups).wait_send()

    for i in range(NZ):
        for way in (0, 1):
            a_copy(i, y, way).wait_send()
            h_copy(i, y, way).wait_send()
        b_copy(i, c).wait_send()

    @pl.loop(0, CHUNKS)
    def _(q):
        @pl.loop(1, 2 * NY)
        def _(step):
            w_copy(q, (t + step) % (2 * NY), t).wait_send()

        for i in range(NZ):
            x_copy(q, i).wait_send()
        for kind in (0, 1):
            for way in (0, 1):
                for s in range(LAST):
                    ring(kind, q, s, way)[4](s).wait_send()
        z_copy(q).wait_send()


def project(hidden, base, gain, down, up, cosine, sine, groups, members):
    width = base.shape[1]
    cols = width // members
    tokens = groups * 128
    tile = cols // CHUNKS // 2
    dma = pltpu.SemaphoreType.DMA
    any_spec = pl.BlockSpec(memory_space=pl.ANY)
    vmem_spec = pl.BlockSpec(memory_space=pltpu.VMEM)
    pair = lambda *shape: [dma(shape), dma(shape)]
    return pl.pallas_call(
        project_kernel,
        in_specs=[any_spec, any_spec] + [vmem_spec] * 5,
        out_specs=vmem_spec,
        out_shape=jax.ShapeDtypeStruct((128, cols), BF16),
        scratch_shapes=[
            pltpu.VMEM((128, width), BF16),
            pltpu.VMEM((128, width), BF16),
            pltpu.VMEM((tokens, 128), BF16),
            pltpu.VMEM((128, width), BF16),
            pltpu.VMEM((tokens, members * BLOCK), BF16),
            pltpu.VMEM((members * BLOCK, cols), BF16),
            pltpu.VMEM((tokens, cols), BF16),
            pltpu.VMEM((CHUNKS, 2, LAST, 256, tile), BF16),
            pltpu.VMEM((CHUNKS, 2, LAST, 128, tile), BF16),
            pltpu.VMEM((CHUNKS, NZ, 128, tile), BF16),
            pltpu.VMEM((CHUNKS, 128, tile), BF16),
            dma((2,)),
            dma((1 + CHUNKS,)),
            *pair(groups),
            *pair(NZ, 2),
            *pair(NZ, 2),
            *pair(NZ),
            *pair(CHUNKS, members),
            *pair(CHUNKS, 2, LAST),
            *pair(CHUNKS, 2, LAST),
            *pair(CHUNKS, NZ),
            *pair(CHUNKS),
        ],
        compiler_params=pltpu.CompilerParams(
            collective_id=0, has_side_effects=True, vmem_limit_bytes=50 * 1024 * 1024
        ),
    )(hidden, base, gain, down, up, cosine, sine)


def solution(mesh):
    groups, members = mesh.shape["fsdp"], mesh.shape["tp"]

    def shards(hidden, base_weight, adapter_down, adapter_up, norm_gain, positions):
        cosine, sine = frequencies(positions)
        return project(
            hidden, base_weight, norm_gain.reshape(-1, 128), adapter_down.T, adapter_up,
            jnp.concatenate([cosine, cosine], axis=1),
            jnp.concatenate([-sine, sine], axis=1),
            groups, members,
        )

    placed = (
        P(("rep", "fsdp"), None),
        P(("rep", "fsdp", "tp"), None),
        P(("rep", "fsdp", "tp"), None),
        P("rep", None),
        P("rep"),
        P(("rep", "fsdp")),
    )
    return jax.shard_map(
        shards, mesh=mesh, in_specs=placed, out_specs=P(("rep", "fsdp"), "tp"), check_vma=False
    )
```

```python
import functools
import math

import jax
import jax.numpy as jnp
from jax import lax
from jax.experimental import pallas as pl
from jax.experimental.pallas import tpu as pltpu
from jax.sharding import PartitionSpec as P

HEAD = 128
BLOCK = 128
F32 = jnp.float32
BF16 = jnp.bfloat16

norm_epsilon = 1e-05
scale_epsilon = 1e-06
code_limit = 15.0
adapter_scale = 2.0
rope_theta = 500000.0
rope_factor = 8.0
low_factor = 1.0
high_factor = 4.0
initial_context = 8192.0

NZ = 8
NY = 4
CHUNKS = 8
STRIDE = 1
LAST = NZ // 2
OFFSETS = (4, 3, -3, 2, -2, 1, -1, 0)
FAR = 5
STEP_BLOCKS = ((0,), (1, 2), (3, 4), (5, 6), (7,))


def frequencies(positions):
    pair_index = jnp.arange(HEAD // 2, dtype=F32)
    inverse = jnp.exp(pair_index * (-2.0 * math.log(rope_theta) / HEAD))
    wavelength = 2.0 * math.pi / inverse
    blend = (initial_context / wavelength - low_factor) / (high_factor - low_factor)
    middle = (1.0 - blend) * inverse / rope_factor + blend * inverse
    adjusted = jnp.where(
        wavelength < initial_context / high_factor,
        inverse,
        jnp.where(wavelength > initial_context / low_factor, inverse / rope_factor, middle),
    )
    angles = positions.astype(F32)[:, None] * adjusted[None, :]
    return (jnp.cos(angles), jnp.sin(angles))


def project_kernel(
    hidden_hbm, base_hbm, gain_ref, down_ref, up_ref, cos_ref, sin_ref, out_ref,
    hidden, base, normed, near, coded, acts, weights, sums, ring_z, ring_x, swap_x, swap_z,
    load_sem, local_sem, n_send, n_recv, a_send, a_recv, h_send, h_recv, b_send, b_recv,
    w_send, w_recv, rz_send, rz_recv, rx_send, rx_recv, sx_send, sx_recv, sz_send, sz_recv,
):
    f = lax.axis_index("fsdp")
    t = lax.axis_index("tp")
    z, x = f // 2, f % 2
    y, c = t // 2, t % 2
    peer_x = {"fsdp": z * 2 + (1 - x)}
    place = c * NY + y
    cols = weights.shape[1]
    cw = cols // CHUNKS
    tile = cw // 2
    groups = 2 * NZ
    width = hidden.shape[1]

    parts = 4
    part_width = width // parts

    def load_hidden(part):
        view = pl.ds(part * part_width, part_width)
        return pltpu.make_async_copy(hidden_hbm.at[:, view], hidden.at[:, view], load_sem.at[part])

    load_base = pltpu.make_async_copy(base_hbm, base, load_sem.at[parts])
    for part in range(parts):
        load_hidden(part).start()

    def zmod(value):
        return (value + NZ) % NZ

    def remote(src, dst, send, recv, device):
        return pltpu.make_async_remote_copy(
            src_ref=src, dst_ref=dst, send_sem=send, recv_sem=recv,
            device_id=device, device_id_type=pl.DeviceIdType.MESH,
        )

    def lane(index, size):
        return pl.ds(pl.multiple_of(index * size, size), size)

    barrier = pltpu.get_barrier_semaphore()

    @pl.loop(1, groups)
    def _(step):
        pl.semaphore_signal(
            barrier, inc=1, device_id={"fsdp": (f + step) % groups},
            device_id_type=pl.DeviceIdType.MESH,
        )

    @pl.loop(1, 2 * NY)
    def _(step):
        pl.semaphore_signal(
            barrier, inc=1, device_id={"tp": (t + step) % (2 * NY)},
            device_id_type=pl.DeviceIdType.MESH,
        )

    span = width // groups

    def squares(group, total):
        values = hidden[:, lane(group, span)].astype(F32)
        for start in range(0, span, 128):
            part = values[:, start : start + 128]
            total = total + part * part
        return total

    total = jnp.zeros((128, 128), F32)
    for part in range(parts):
        load_hidden(part).wait()
        if part == parts - 1:
            load_base.start()
        total = lax.fori_loop(
            part * (groups // parts), (part + 1) * (groups // parts), squares, total
        )
    mean_square = jnp.sum(total, axis=1, keepdims=True) / width
    members = 2 * NY
    factor = jnp.broadcast_to(lax.rsqrt(mean_square + norm_epsilon), (128, 128))
    row_index = lax.broadcasted_iota(jnp.int32, (members, 128), 0)

    def normalized(group, member):
        gains = gain_ref[lane(group, members), :].astype(F32)
        gain = jnp.sum(jnp.where(row_index == member, gains, 0.0), axis=0, keepdims=True)
        values = hidden[:, lane(group * members + member, 128)].astype(F32)
        return (values * factor * gain).astype(BF16)

    @pl.loop(0, groups)
    def _(group):
        normed[lane(group, 128), :] = normalized(group, t)

    pl.semaphore_wait(barrier, groups - 1 + 2 * NY - 1)

    def n_copy(source, target):
        return remote(
            normed.at[lane(target, 128), :], acts.at[lane(source, 128), lane(place, 128)],
            n_send.at[target], n_recv.at[source], {"fsdp": target},
        )

    def near_copy(n, source, target):
        return remote(
            near.at[n], acts.at[lane(source, 128), lane(c, 128 * NY)],
            n_send.at[target], n_recv.at[source], {"fsdp": target},
        )

    def far_targets():
        return [zmod(z - off) * 2 + (x + flip) % 2 for off in OFFSETS[:FAR] for flip in (0, 1)]

    def near_targets():
        ends = [(1, 0), (1, 1), (-1, 0), (-1, 1), (0, 1)]
        return [zmod(z + dz) * 2 + (x + flip) % 2 for dz, flip in ends]

    for target in far_targets():
        n_copy(f, target).start()

    def near_start():
        for n, target in enumerate(near_targets()):
            near[n] = jnp.concatenate([normalized(target, 2 * k + c) for k in range(NY)], axis=1)
            near_copy(n, f, target).start()
        for member in range(members):
            column = ((member % 2) * NY + member // 2) * 128
            acts[lane(f, 128), column : column + 128] = normalized(f, member)

    def w_copy(q, target, source):
        row = (source % 2) * NY + source // 2
        return remote(
            coded.at[:, pl.ds(pl.multiple_of(target * cols + q * cw, cw), cw)],
            weights.at[lane(row, BLOCK), lane(q, cw)],
            w_send.at[q, target], w_recv.at[q, source], {"tp": target},
        )

    def w_own(q):
        return pltpu.make_async_copy(
            coded.at[:, pl.ds(pl.multiple_of(t * cols + q * cw, cw), cw)],
            weights.at[lane(place, BLOCK), lane(q, cw)], local_sem.at[1 + q],
        )

    def w_start(q):
        doubled = down_ref[...] * adapter_scale
        views, merged, maxima = [], [], []
        for target in range(2 * NY):
            here = pl.ds(pl.multiple_of(target * cols + q * cw, cw), cw)
            low_rank = lax.dot_general(
                doubled, up_ref[:, here], (((0,), (0,)), ((), ())), preferred_element_type=F32
            )
            value = base[:, here].astype(F32) + low_rank
            by_column = jnp.max(jnp.abs(value), axis=0, keepdims=True)
            views.append(here)
            merged.append(value)
            maxima += [by_column[:, start : start + BLOCK] for start in range(0, cw, BLOCK)]
        stacked = jnp.concatenate(maxima, axis=0)
        largest = jnp.max(stacked, axis=1, keepdims=True) + scale_epsilon
        largest = jnp.broadcast_to(largest, stacked.shape)
        scale = jnp.full(stacked.shape, 2.0**-23, F32)
        inverse = jnp.full(stacked.shape, 2.0**23, F32)
        for power in range(-23, 1):
            above = largest > code_limit * 2.0**power
            scale = jnp.where(above, 2.0 ** (power + 1), scale)
            inverse = jnp.where(above, 2.0 ** -(power + 1), inverse)
        for target in range(2 * NY):
            result = []
            for part in range(cw // BLOCK):
                row = target * (cw // BLOCK) + part
                block = merged[target][:, part * BLOCK : (part + 1) * BLOCK]
                codes = jnp.floor(block * inverse[row : row + 1] + 0.5)
                result.append((codes * scale[row : row + 1]).astype(BF16))
            coded[:, views[target]] = jnp.concatenate(result, axis=1)

        for dy, dc in ((1, 0), (3, 0), (1, 1), (3, 1), (2, 0), (2, 1), (0, 1)):
            w_copy(q, ((y + dy) % NY) * 2 + (c + dc) % 2, t).start()
        w_own(q).start()

    def rows_of(i):
        return lane(zmod(z + OFFSETS[i]), 256)

    def a_copy(i, source_y, way):
        view = acts.at[rows_of(i), lane(c * NY + source_y, 128)]
        target = (y + (1 if way == 0 else NY - 1)) % NY
        return remote(view, view, a_send.at[i, way], a_recv.at[i, way], {"tp": target * 2 + c})

    def h_copy(i, source_y, way):
        rows = pl.ds(pl.multiple_of(zmod(z + OFFSETS[i]) * 256 + way * 128, 128), 128)
        view = acts.at[rows, lane(c * NY + source_y, 128)]
        target = (y + (1 if way == 0 else NY - 1)) % NY
        return remote(view, view, h_send.at[i, way], h_recv.at[i, way], {"tp": target * 2 + c})

    def b_copy(i, half):
        rows = rows_of(i)
        if i == NZ - 1:
            rows = pl.ds(pl.multiple_of(z * 256 + (1 - x) * 128, 128), 128)
        view = acts.at[rows, lane(half, 128 * NY)]
        return remote(view, view, b_send.at[i], b_recv.at[i], {"tp": y * 2 + 1 - c})

    down_y, up_y, far_y = (y + NY - 1) % NY, (y + 1) % NY, (y + 2) % NY

    def stage_a(i):
        for other in (0, 1):
            n_copy(zmod(z + OFFSETS[i]) * 2 + other, f).wait_recv()
        for way in (0, 1):
            a_copy(i, y, way).start()

    def stage_h(i):
        for way, source in ((0, down_y), (1, up_y)):
            a_copy(i, source, way).wait_recv()
            h_copy(i, source, way).start()

    def stage_b(i):
        if i < FAR:
            for way in (0, 1):
                h_copy(i, far_y, way).wait_recv()
        elif OFFSETS[i]:
            for other in (0, 1):
                near_copy(0, zmod(z + OFFSETS[i]) * 2 + other, f).wait_recv()
        else:
            near_copy(0, z * 2 + 1 - x, f).wait_recv()
        b_copy(i, c).start()

    def stage_c(i):
        b_copy(i, 1 - c).wait_recv()

    def x_copy(q, i):
        rows = pl.ds(pl.multiple_of(zmod(z + OFFSETS[i]) * 256 + (1 - x) * 128, 128), 128)
        here = pl.ds(pl.multiple_of(q * cw + tile, tile), tile)
        return remote(
            sums.at[rows, here], swap_x.at[q, i], sx_send.at[q, i], sx_recv.at[q, i], peer_x
        )

    def products(q, s):
        for i in STEP_BLOCKS[s]:
            value = jnp.dot(
                acts[rows_of(i), :], weights[:, lane(q, cw)], preferred_element_type=F32
            )
            sums[rows_of(i), lane(q, cw)] = value.astype(BF16)
            x_copy(q, i).start()

    def finish(q, which, value):
        turned = value * cos_ref[...] + pltpu.roll(value, HEAD // 2, 1) * sin_ref[...]
        out_ref[:, pl.ds(pl.multiple_of(q * cw + which * tile, tile), tile)] = turned.astype(BF16)

    def z_copy(q):
        rows = pl.ds(pl.multiple_of(z * 256 + (1 - x) * 128, 128), 128)
        return remote(
            sums.at[rows, pl.ds(pl.multiple_of(q * cw, cw), tile)],
            swap_z.at[q], sz_send.at[q], sz_recv.at[q], peer_x,
        )

    def ring(kind, q, s, way):
        size = 256 if kind == 0 else 128
        block = zmod(z + (LAST - s)) if way == 0 else zmod(z - (LAST - s))
        first = block * 256 if kind == 0 else block * 256 + x * 128
        here = pl.ds(pl.multiple_of(q * cw + kind * tile, tile), tile)
        slots, sends, recvs = (
            (ring_z, rz_send, rz_recv) if kind == 0 else (ring_x, rx_send, rx_recv)
        )
        target = zmod(z + 1) if way == 0 else zmod(z - 1)

        def hop(step):
            if step == 0:
                half = size // 2
                src = sums.at[pl.ds(pl.multiple_of(first + way * half, half), half), here]
                dst = slots.at[q, way, 0, pl.ds(0, half)]
            else:
                src = sums.at[pl.ds(pl.multiple_of(first, size), size), here]
                dst = slots.at[q, way, step]
            return remote(
                src, dst, sends.at[q, way, step], recvs.at[q, way, step],
                {"fsdp": target * 2 + x},
            )

        return size, first, here, slots, hop

    def ring_step(kind, q, s):
        size, first, here, slots, hop = ring(kind, q, s, 0)
        half = size // 2

        def read(start, count):
            rows = pl.ds(pl.multiple_of(start, count), count)
            return sums[rows, here]

        def put(start, count, value):
            sums[pl.ds(pl.multiple_of(start, count), count), here] = value.astype(BF16)

        def swapped(i, start=0, count=size):
            return swap_x[q, i, start : start + count]

        if kind == 1:
            for i in STEP_BLOCKS[s]:
                x_copy(q, i).wait_recv()
        if s == 0:
            if kind == 1:
                put(first, size, read(first, size) + swapped(0))
            for way in (0, 1):
                ring(kind, q, s, way)[4](0).start()
        elif s < LAST:
            for way in (0, 1):
                size, first, here, slots, hop = ring(kind, q, s, way)
                i = STEP_BLOCKS[s][way]
                hop(s - 1).wait_recv()
                if s == 1:
                    middle = first + way * half
                    value = read(middle, half) + slots[q, way, 0, 0:half]
                    if kind == 1:
                        value = value + swapped(i, way * half, half)
                        other = first + (1 - way) * half
                        put(other, half, read(other, half) + swapped(i, (1 - way) * half, half))
                    put(middle, half, value)
                else:
                    value = read(first, size) + slots[q, way, s - 1]
                    if kind == 1:
                        value = value + swapped(i)
                    put(first, size, value)
                hop(s).start()
        else:
            value = read(first, size).astype(F32)
            if kind == 1:
                value = value + swapped(7).astype(F32)
            for way in (0, 1):
                ring(kind, q, s, way)[4](s - 1).wait_recv()
                value = value + slots[q, way, s - 1].astype(F32)
            if kind == 0:
                put(first, size, value)
                z_copy(q).start()
            else:
                finish(q, 1, value)

    def last_z(q):
        z_copy(q).wait_recv()
        rows = pl.ds(pl.multiple_of(z * 256 + x * 128, 128), 128)
        here = pl.ds(pl.multiple_of(q * cw, cw), tile)
        finish(q, 0, sums[rows, here].astype(F32) + swap_z[q].astype(F32))

    load_base.wait()
    w_start(0)
    near_start()
    stage_a(0)
    w_start(1)
    stage_a(1), stage_a(2), stage_h(0)
    stage_a(3), stage_a(4), stage_h(1), stage_h(2), stage_b(0)
    stage_h(3), stage_h(4), stage_b(1), stage_b(2)
    w_start(2), w_start(3)
    stage_b(3), stage_b(4)

    def at_chunk(start, run):
        @pl.when((start >= 0) & (start % STRIDE == 0) & (start < STRIDE * CHUNKS))
        def _():
            run(start // STRIDE)

    def arrive(q):
        w_own(q).wait()

        @pl.loop(1, 2 * NY)
        def _(step):
            w_copy(q, t, (t + step) % (2 * NY)).wait_recv()

    @pl.loop(0, STRIDE * (CHUNKS - 1) + LAST + 3)
    def _(r):
        at_chunk(r - LAST - 2, last_z)
        for s in range(LAST, -1, -1):
            at_chunk(r - s - 1, functools.partial(ring_step, 0, s=s))
            at_chunk(r - s - 2, functools.partial(ring_step, 1, s=s))

            @pl.when(r == s)
            def _():
                for i in STEP_BLOCKS[s]:
                    stage_c(i)

            if s == 0:
                at_chunk(r, arrive)
            at_chunk(r - s, functools.partial(products, s=s))

        @pl.when(r == 1)
        def _():
            stage_b(5), stage_b(6), stage_b(7)

        @pl.when(r + 4 < CHUNKS)
        def _():
            w_start(r + 4)

    for target in far_targets():
        n_copy(f, target).wait_send()
    for n, target in enumerate(near_targets()):
        near_copy(n, f, target).wait_send()
    for i in range(NZ):
        if i < FAR:
            for way in (0, 1):
                a_copy(i, y, way).wait_send()
                h_copy(i, y, way).wait_send()
        b_copy(i, c).wait_send()

    @pl.loop(0, CHUNKS)
    def _(q):
        @pl.loop(1, 2 * NY)
        def _(step):
            w_copy(q, (t + step) % (2 * NY), t).wait_send()

        for i in range(NZ):
            x_copy(q, i).wait_send()
        for kind in (0, 1):
            for way in (0, 1):
                for s in range(LAST):
                    ring(kind, q, s, way)[4](s).wait_send()
        z_copy(q).wait_send()


def project(hidden, base, gain, down, up, cosine, sine, groups, members):
    width = base.shape[1]
    cols = width // members
    tokens = groups * 128
    tile = cols // CHUNKS // 2
    dma = pltpu.SemaphoreType.DMA
    any_spec = pl.BlockSpec(memory_space=pl.ANY)
    vmem_spec = pl.BlockSpec(memory_space=pltpu.VMEM)
    pair = lambda *shape: [dma(shape), dma(shape)]
    return pl.pallas_call(
        project_kernel,
        in_specs=[any_spec, any_spec] + [vmem_spec] * 5,
        out_specs=vmem_spec,
        out_shape=jax.ShapeDtypeStruct((128, cols), BF16),
        scratch_shapes=[
            pltpu.VMEM((128, width), BF16),
            pltpu.VMEM((128, width), BF16),
            pltpu.VMEM((tokens, 128), BF16),
            pltpu.VMEM((NZ - 3, 128, 128 * NY), BF16),
            pltpu.VMEM((128, width), BF16),
            pltpu.VMEM((tokens, members * BLOCK), BF16),
            pltpu.VMEM((members * BLOCK, cols), BF16),
            pltpu.VMEM((tokens, cols), BF16),
            pltpu.VMEM((CHUNKS, 2, LAST, 256, tile), BF16),
            pltpu.VMEM((CHUNKS, 2, LAST, 128, tile), BF16),
            pltpu.VMEM((CHUNKS, NZ, 128, tile), BF16),
            pltpu.VMEM((CHUNKS, 128, tile), BF16),
            dma((5,)),
            dma((1 + CHUNKS,)),
            *pair(groups),
            *pair(NZ, 2),
            *pair(NZ, 2),
            *pair(NZ),
            *pair(CHUNKS, members),
            *pair(CHUNKS, 2, LAST),
            *pair(CHUNKS, 2, LAST),
            *pair(CHUNKS, NZ),
            *pair(CHUNKS),
        ],
        compiler_params=pltpu.CompilerParams(
            collective_id=0, has_side_effects=True, vmem_limit_bytes=56 * 1024 * 1024
        ),
    )(hidden, base, gain, down, up, cosine, sine)


def solution(mesh):
    groups, members = mesh.shape["fsdp"], mesh.shape["tp"]

    def shards(hidden, base_weight, adapter_down, adapter_up, norm_gain, positions):
        cosine, sine = frequencies(positions)
        return project(
            hidden, base_weight, norm_gain.reshape(-1, 128), adapter_down.T, adapter_up,
            jnp.concatenate([cosine, cosine], axis=1),
            jnp.concatenate([-sine, sine], axis=1),
            groups, members,
        )

    placed = (
        P(("rep", "fsdp"), None),
        P(("rep", "fsdp", "tp"), None),
        P(("rep", "fsdp", "tp"), None),
        P("rep", None),
        P("rep"),
        P(("rep", "fsdp")),
    )
    return jax.shard_map(
        shards, mesh=mesh, in_specs=placed, out_specs=P(("rep", "fsdp"), "tp"), check_vma=False
    )
```
